256 devices in a mesh: pool: 32 (over y, z), head: 8 (over x, core).
Axes of the slice: x: 4, y: 4, z: 8, core: 2. Of those that a mesh axis runs over, the one named last changes fastest.
Arguments:
- queries: bfloat16 [32, 256, 8192], P('pool', None, 'head'), may hold values from -6 to 6
- new_kv: bfloat16 [32, 256, 2048], P('pool', None, 'head'), may hold values from -6 to 6
- pool: bfloat16 [1024, 256, 2048], P('pool', None, 'head'), may hold values from -6 to 6
- page_owner: int32 [32, 32], replicated, may hold values from 0 to 31, as said below
- page_slot: int32 [32, 32], replicated, may hold values from 0 to 31, as said below
- cached_len: int32 [32], replicated, may hold values from 1 to 8192, as said below
Outputs:
- attended: bfloat16 [32, 256, 8192], P('pool', None, 'head')
The draws below stay inside these ranges and needn't reach their ends.
Inputs may be any that keep to these rules, and one draw needn't show every extreme that they name: `page_owner`: each of the 32 entries of a row is the owner of that page of the request; every owner holds exactly 1 entries of each row. Pairs (page_owner, page_slot) are distinct over all requests and pages. Request r uses its first ceil(cached_len[r] / 256) pages; some request has exactly 8192 cached tokens.
All inputs are finite; a program needn't handle non-finite values.
Results may differ from the reference program's by a relative error of at most 0.0075.
Values may be sent and summed in bfloat16 or wider, within the bound.
No kernel may reach another device: no remote copies, remote signals or barrier semaphores. Data moves between devices by JAX's collectives and lax.ppermute only.
A program may use at most 64 MiB of HBM per device.

```python
import math
import jax
import jax.numpy as jnp
from jax import lax

QH = 64
KVH = 8
HD = 128
PAGE = 256
MAXPG = 32
NEW = 256
REQS = 32
PAGES_DEV = 32
CTX = 8192
N_POOL = 32


def page_tables(key):
    perm_key = jax.random.fold_in(key, 21)
    slot_key = jax.random.fold_in(key, 22)
    owner_perm = jax.vmap(lambda subkey: jax.random.permutation(subkey, N_POOL))(jax.random.split(perm_key, REQS))
    slot_perm = jax.vmap(lambda subkey: jax.random.permutation(subkey, PAGES_DEV))(jax.random.split(slot_key, N_POOL))
    per_owner = MAXPG // N_POOL
    page_numbers = jnp.arange(MAXPG, dtype=jnp.int32)
    owners = owner_perm[:, page_numbers % N_POOL]
    local_rank = jnp.arange(REQS, dtype=jnp.int32)[:, None] * per_owner + (page_numbers // N_POOL)[None, :]
    slots = slot_perm[owners, local_rank]
    return (owners.astype(jnp.int32), slots.astype(jnp.int32))


def draw_page_owner(key, part):
    return page_tables(key)[0]


def draw_page_slot(key, part):
    return page_tables(key)[1]


def draw_cached_len(key, part):
    lengths = jax.random.randint(jax.random.fold_in(key, 31), (REQS,), 1, MAXPG * PAGE + 1)
    longest = jax.random.randint(jax.random.fold_in(key, 32), (), 0, REQS)
    lengths = jnp.where(jnp.arange(REQS) == longest, MAXPG * PAGE, lengths)
    return lengths.astype(jnp.int32)


def draw_queries(key, part):
    sample_key = jax.random.fold_in(key, 11)
    shape = (REQS, NEW, QH * HD)
    sample = jnp.clip(jax.random.normal(sample_key, shape, jnp.float32), -6.0, 6.0)
    return sample.astype(jnp.bfloat16)


def draw_pool(key, part):
    sample_key = jax.random.fold_in(key, 12)
    shape = (N_POOL * PAGES_DEV, PAGE, KVH * 2 * HD)
    sample = jnp.clip(jax.random.normal(sample_key, shape, jnp.float32), -6.0, 6.0)
    return sample.astype(jnp.bfloat16)


def levels(own_key, shape, shards, low, high):
    def one(position, blocks):
        heights = jax.random.uniform(jax.random.fold_in(jax.random.fold_in(own_key, 6), position), (blocks,), jnp.float32, low / len(shards), high / len(shards))
        return jnp.repeat(jnp.exp(heights), shape[position] // blocks).reshape((-1,) + (1,) * (len(shape) - position - 1))

    level = one(*shards[0])
    for cut in shards[1:]:
        level = level * one(*cut)
    return level


def noise(stream_key, extent, width, reach, cuts=(), kind=jnp.bfloat16):
    gain = levels(stream_key, extent, cuts, -0.22, 0.18) if cuts else 1.0
    values = jax.random.normal(stream_key, extent, jnp.float32) * width * gain
    return jnp.minimum(jnp.maximum(values, -reach), reach).astype(kind)


def setup_inputs(seed: int = 0) -> dict:
    streams_of = jax.random.split(jax.random.key(seed), 7)
    return {
        "queries": draw_queries(jax.random.fold_in(streams_of[6], 71), 0),
        "new_kv": noise(streams_of[1], (REQS, NEW, KVH * 2 * HD), 1.0, 6.0, ((0, 32), (2, 8))),
        "pool": draw_pool(jax.random.fold_in(streams_of[6], 71), 0),
        "page_owner": draw_page_owner(jax.random.fold_in(streams_of[6], 71), 0),
        "page_slot": draw_page_slot(jax.random.fold_in(streams_of[6], 71), 0),
        "cached_len": draw_cached_len(jax.random.fold_in(streams_of[6], 71), 0),
    }


def reference(queries, new_kv, pool, page_owner, page_slot, cached_len):
    group_size = QH // KVH
    score_scale = 1.0 / math.sqrt(HD)
    positions = jnp.arange(CTX + NEW, dtype=jnp.int32)
    tokens_now = jnp.arange(NEW, dtype=jnp.int32)

    def one_request(request_no):
        query_rows = queries[request_no].reshape(NEW, KVH, group_size, HD)
        page_ids = (page_owner[request_no] * PAGES_DEV + page_slot[request_no]).astype(jnp.int32)
        cached = jnp.take(pool, page_ids, axis=0).reshape(MAXPG * PAGE, KVH, 2, HD)
        fresh = new_kv[request_no].reshape(NEW, KVH, 2, HD)
        key_rows = jnp.concatenate([cached[:, :, 0], fresh[:, :, 0]], axis=0)
        value_rows = jnp.concatenate([cached[:, :, 1], fresh[:, :, 1]], axis=0)
        cached_seen = (positions < cached_len[request_no])[None, :]
        fresh_seen = (positions - CTX)[None, :] <= tokens_now[:, None]
        visible = jnp.where((positions < CTX)[None, :], cached_seen, fresh_seen)

        def one_head(head_no):
            head_query = query_rows[:, head_no].astype(jnp.float32)
            head_keys = key_rows[:, head_no].astype(jnp.float32)
            scores = jnp.einsum('igd,kd->gik', head_query, head_keys) * score_scale
            scores = jnp.where(visible[None], scores, -jnp.inf)
            row_peak = lax.optimization_barrier(jnp.max(scores, axis=-1, keepdims=True))
            numer = jnp.exp(scores - row_peak)
            row_total = lax.optimization_barrier(jnp.sum(numer, axis=-1))
            weights = numer.astype(jnp.bfloat16)
            result = jnp.einsum('gik,kd->gid', weights.astype(jnp.float32), value_rows[:, head_no].astype(jnp.float32))
            return result / row_total[..., None]
        heads_out = lax.map(one_head, jnp.arange(KVH, dtype=jnp.int32))
        return heads_out.transpose(2, 0, 1, 3).reshape(NEW, QH * HD).astype(jnp.bfloat16)
    return lax.map(one_request, jnp.arange(REQS, dtype=jnp.int32))
```

```python
import math

import jax
import jax.numpy as jnp
from jax import lax
from jax.experimental import pallas as pl
from jax.experimental.pallas import tpu as pltpu
from jax.sharding import PartitionSpec as P


HD = 128
PAGE = 256
NY = 4
NZ = 8
SCALE = math.log2(math.e) / math.sqrt(HD)
MASKED = -1e30


def gather_pages(pool, slots, counts):
    total = sum(counts)

    def body(slot_ref, pool_ref, *refs):
        outs, sem = refs[:-1], refs[-1]
        copies = []
        k = 0
        for out, count in zip(outs, counts):
            for i in range(count):
                copies.append(
                    pltpu.make_async_copy(pool_ref.at[slot_ref[k]], out.at[i], sem.at[k])
                )
                k += 1
        for c in copies:
            c.start()
        for c in copies:
            c.wait()

    return pl.pallas_call(
        body,
        grid_spec=pltpu.PrefetchScalarGridSpec(
            num_scalar_prefetch=1,
            grid=(1,),
            in_specs=[pl.BlockSpec(memory_space=pl.ANY)],
            out_specs=[
                pl.BlockSpec((c,) + pool.shape[1:], lambda g, l: (0, 0, 0)) for c in counts
            ],
            scratch_shapes=[pltpu.SemaphoreType.DMA((total,))],
        ),
        out_shape=[jax.ShapeDtypeStruct((c,) + pool.shape[1:], pool.dtype) for c in counts],
    )(slots, pool)


def attend(q, state, lims, pieces, fresh, final, wide=False):
    heads = q.shape[1] // HD
    rows = q.shape[0]
    npg = sum(c for _, _, c in pieces)
    lead = 1 if fresh is not None else 0
    nkv = npg + lead
    has_state = state is not None

    def body(lim_ref, q_ref, *refs):
        refs = list(refs)
        st_in = refs.pop(0) if has_state else None
        fr = refs.pop(0) if lead else None
        pgs = [refs.pop(0) for _ in pieces]
        out = refs.pop(0)
        k_ref, v_ref = refs
        v_ref[:, HD:] = jnp.ones((nkv * PAGE, HD), jnp.bfloat16)
        blocks = [fr[...]] if lead else []
        for pg, (_, first, count) in zip(pgs, pieces):
            blocks += [pg[first + i] for i in range(count)]
        for i, blk in enumerate(blocks):
            at = i * PAGE
            k_ref[at : at + PAGE, :HD] = blk[:, :HD]
            if wide:
                k_ref[at : at + PAGE, HD:] = blk[:, :HD]
            v_ref[at : at + PAGE, :HD] = blk[:, HD:]
        lane = lax.broadcasted_iota(jnp.int32, (1, PAGE), 1)
        bias = [jnp.where(lane < lim_ref[i], 0.0, MASKED) for i in range(npg)]
        half = lax.broadcasted_iota(jnp.int32, (rows, HD), 1) < HD // 2
        for h in range(heads):
            qh = q_ref[:, h * HD : (h + 1) * HD]
            if wide:
                qf = qh.astype(jnp.float32) * SCALE
                hi = qf.astype(jnp.bfloat16)
                lo = (qf - hi.astype(jnp.float32)).astype(jnp.bfloat16)
                qh = jnp.concatenate([hi, lo], axis=1)
            s = lax.dot_general(
                qh, k_ref[...], (((1,), (1,)), ((), ())), preferred_element_type=jnp.float32
            )
            if not wide:
                s = s * SCALE
            cols = []
            for i in range(nkv):
                c = s[:, i * PAGE : (i + 1) * PAGE]
                if i < lead:
                    r_i = lax.broadcasted_iota(jnp.int32, (rows, PAGE), 0)
                    c_i = lax.broadcasted_iota(jnp.int32, (rows, PAGE), 1)
                    c = jnp.where(c_i <= r_i, c, MASKED)
                else:
                    c = c + bias[i - lead]
                cols.append(c)
            s = jnp.concatenate(cols, axis=1) if nkv > 1 else cols[0]
            peak = jnp.max(s, axis=-1, keepdims=True)
            if has_state:
                old = st_in[h]
                old_peak = old[:, 2 * HD - 1 :]
                peak = jnp.maximum(peak, old_peak)
                shrink = jnp.exp2(old_peak - peak)
            w = jnp.exp2(s - peak).astype(jnp.bfloat16)
            acc = jnp.dot(w, v_ref[...], preferred_element_type=jnp.float32)
            if has_state:
                acc = acc + old * shrink
            if final:
                out[:, h * HD : (h + 1) * HD] = (acc[:, :HD] / acc[:, HD : HD + 1]).astype(
                    jnp.bfloat16
                )
            else:
                out[h, :, :HD] = acc[:, :HD]
                out[h, :, HD:] = jnp.where(half, acc[:, HD:], peak)

    args = [q]
    if has_state:
        args.append(state)
    if lead:
        args.append(fresh)
    args += [arr for arr, _, _ in pieces]
    whole = pl.BlockSpec(memory_space=pltpu.VMEM)
    if final:
        out_shape = jax.ShapeDtypeStruct(q.shape, jnp.bfloat16)
    else:
        out_shape = jax.ShapeDtypeStruct((heads, rows, 2 * HD), jnp.float32)
    return pl.pallas_call(
        body,
        in_specs=[pl.BlockSpec(memory_space=pltpu.SMEM)] + [whole] * len(args),
        out_specs=whole,
        scratch_shapes=[
            pltpu.VMEM((nkv * PAGE, 2 * HD if wide else HD), jnp.bfloat16),
            pltpu.VMEM((nkv * PAGE, 2 * HD), jnp.bfloat16),
        ],
        out_shape=out_shape,
        input_output_aliases={2: 0} if has_state and not final else {},
        compiler_params=pltpu.CompilerParams(vmem_limit_bytes=48 << 20),
    )(lims, *args)


def shift(x, dy, dz):
    pairs = [
        (s, ((s // NZ + dy) % NY) * NZ + (s % NZ + dz) % NZ) for s in range(NY * NZ)
    ]
    return lax.ppermute(x, "pool", pairs)


NEAR = (2, -2, 1, -1)


def on_device(queries, new_kv, pool, page_owner, page_slot, cached_len):
    me = lax.axis_index("pool")
    y = me >> 3
    z = me & (NZ - 1)
    q = queries[0]

    def at(moves, sign):
        table = jnp.array(moves, jnp.int32) * sign
        return ((y + table[:, 0]) & (NY - 1)) * NZ + ((z + table[:, 1]) & (NZ - 1))

    lead = [(dy, dz) for dz in (3, -3, 4) for dy in range(NY)]
    side = [(dy, dz) for dy in (1, 2, 3) for dz in (0, 2, -2, 1, -1)]
    mine = [(0, 0)] + [(0, dz) for dz in NEAR]
    order = lead + side + mine
    out_req = at(order, 1)
    owned = page_owner == me
    slot_of = jnp.sum(jnp.where(owned, page_slot, 0), axis=1)
    pick = out_req[:, None] == jnp.arange(NY * NZ, dtype=jnp.int32)[None, :]
    slots = jnp.sum(jnp.where(pick, slot_of[None, :], 0), axis=1)

    in_order = [(0, 0), (1, 0), (2, 0), (3, 0)]
    in_order += [(0, 3), (0, -3)] + [(dy, dz) for dy in (1, 2, 3) for dz in (3, -3)]
    in_order += [(dy, 4) for dy in range(NY)]
    for dz in NEAR:
        in_order += [(dy, dz) for dy in range(NY)]
    owners = at(in_order, -1)
    own_row = lax.dynamic_index_in_dim(page_owner, me, 0, keepdims=False)
    number = jnp.arange(own_row.shape[0], dtype=jnp.int32)
    page_no = jnp.sum(
        jnp.where(owners[:, None] == own_row[None, :], number[None, :], 0), axis=1
    )
    lims = jnp.clip(cached_len[me] - PAGE * page_no, 0, PAGE).astype(jnp.int32)

    z3p, z3m, z4 = gather_pages(pool, slots[:12], (4, 4, 4))
    y1, y2, y3 = gather_pages(pool, slots[12:27], (5, 5, 5))
    m0, m2p, m2m, m1p, m1m = gather_pages(pool, slots[27:], (1, 1, 1, 1, 1))

    r3p, r3m = shift(z3p, 0, 3), shift(z3m, 0, -3)
    r4 = shift(z4, 0, 4)
    s1, s3, s2 = shift(y1, 1, 0), shift(y3, 3, 0), shift(y2, 2, 0)

    near = []
    for k, own in enumerate((m2p, m2m, m1p, m1m)):
        bundle = jnp.concatenate([own] + [s[k + 1 : k + 2] for s in (s1, s2, s3)], axis=0)
        near.append(shift(bundle, 0, NEAR[k]))
    r2p, r2m, r1p, r1m = near

    f = [
        shift(jnp.concatenate([r3p[dy : dy + 1], r3m[dy : dy + 1]], axis=0), dy, 0)
        for dy in (1, 2, 3)
    ]
    g = [shift(r4[dy : dy + 1], dy, 0) for dy in (1, 2, 3)]

    state = attend(
        q, None, lims[0:4], [(m0, 0, 1), (s1, 0, 1), (s2, 0, 1), (s3, 0, 1)], new_kv[0], False
    )
    state = attend(
        q, state, lims[4:12],
        [(r3p, 0, 1), (r3m, 0, 1), (f[0], 0, 2), (f[1], 0, 2), (f[2], 0, 2)], None, False,
    )
    state = attend(
        q, state, lims[12:16], [(r4, 0, 1), (g[0], 0, 1), (g[1], 0, 1), (g[2], 0, 1)], None, False
    )
    state = attend(q, state, lims[16:24], [(r2p, 0, 4), (r2m, 0, 4)], None, False)
    out = attend(q, state, lims[24:32], [(r1p, 0, 4), (r1m, 0, 4)], None, True)
    return out[None]


def solution(mesh):
    split = P("pool", None, "head")
    return jax.shard_map(
        on_device,
        mesh=mesh,
        in_specs=(split, split, split, P(), P(), P()),
        out_specs=split,
        check_vma=False,
    )
```

```python
import math

import jax
import jax.numpy as jnp
from jax import lax
from jax.experimental import pallas as pl
from jax.experimental.pallas import tpu as pltpu
from jax.sharding import PartitionSpec as P


HD = 128
PAGE = 256
NY = 4
NZ = 8
SCALE = math.log2(math.e) / math.sqrt(HD)
MASKED = -1e30


def gather_pages(pool, slots, base, counts):
    def body(slot_ref, pool_ref, *outs):
        places = [(out, i) for out, count in zip(outs, counts) for i in range(count)]
        for k, (out, i) in enumerate(places):
            out[i] = pool_ref[slot_ref[base + k]]

    whole = pl.BlockSpec(memory_space=pltpu.VMEM)
    return pl.pallas_call(
        body,
        in_specs=[pl.BlockSpec(memory_space=pltpu.SMEM), whole],
        out_specs=[whole] * len(counts),
        out_shape=[jax.ShapeDtypeStruct((c,) + pool.shape[1:], pool.dtype) for c in counts],
        compiler_params=pltpu.CompilerParams(vmem_limit_bytes=4 << 20),
    )(slots, pool)


def bundles(arrays, plans):
    plans = [
        [(i, p[0]) for i in range(len(arrays))] if len(p) == 1 else list(p) for p in plans
    ]

    def body(*refs):
        ins, outs = refs[: len(arrays)], refs[len(arrays) :]
        for out, plan in zip(outs, plans):
            for at, (i, k) in enumerate(plan):
                out[at] = ins[i][k]

    whole = pl.BlockSpec(memory_space=pltpu.VMEM)
    return pl.pallas_call(
        body,
        in_specs=[whole] * len(arrays),
        out_specs=[whole] * len(plans),
        out_shape=[
            jax.ShapeDtypeStruct((len(p),) + arrays[0].shape[1:], arrays[0].dtype) for p in plans
        ],
        compiler_params=pltpu.CompilerParams(vmem_limit_bytes=4 << 20),
    )(*arrays)


def attend(q, state, lims, base, pieces, fresh, mode, unroll=8):
    heads = q.shape[1] // HD
    rows = q.shape[0]
    npg = sum(len(ids) for _, ids in pieces)
    lead = 1 if fresh is not None else 0
    nkv = npg + lead
    has_state = state is not None

    def body(lim_ref, q_ref, *refs):
        refs = list(refs)
        st_in = refs.pop(0) if has_state else None
        fr = refs.pop(0) if lead else None
        pgs = [refs.pop(0) for _ in pieces]
        out = refs.pop(0)
        k_ref, v_ref, stat_ref = refs
        v_ref[:, HD:] = jnp.ones((nkv * PAGE, HD), jnp.bfloat16)
        blocks = [fr[...]] if lead else []
        for pg, (_, ids) in zip(pgs, pieces):
            blocks += [pg[i] for i in ids]
        for i, blk in enumerate(blocks):
            at = i * PAGE
            k_ref[at : at + PAGE] = blk[:, :HD]
            v_ref[at : at + PAGE, :HD] = blk[:, HD:]
        lane = lax.broadcasted_iota(jnp.int32, (1, PAGE), 1)
        bias = [jnp.where(lane < lim_ref[base + i], 0.0, MASKED) for i in range(npg)]
        lanes = lax.broadcasted_iota(jnp.int32, (rows, HD), 1)
        if mode != "state":
            stat_ref[...] = jnp.zeros((rows, HD), jnp.float32)

        def one_head(h):
            at = pl.multiple_of(h * HD, HD)
            qh = q_ref[:, pl.ds(at, HD)]
            s = lax.dot_general(
                qh, k_ref[...], (((1,), (1,)), ((), ())), preferred_element_type=jnp.float32
            )
            cols = []
            for i in range(nkv):
                c = s[:, i * PAGE : (i + 1) * PAGE] * SCALE
                if i < lead:
                    r_i = lax.broadcasted_iota(jnp.int32, (rows, PAGE), 0)
                    c_i = lax.broadcasted_iota(jnp.int32, (rows, PAGE), 1)
                    c = jnp.where(c_i <= r_i, c, MASKED)
                else:
                    c = c + bias[i - lead]
                cols.append(c)
            s = jnp.concatenate(cols, axis=1) if nkv > 1 else cols[0]
            peak = jnp.max(s, axis=-1, keepdims=True)
            if has_state:
                old = st_in[h]
                old_peak = old[:, 2 * HD - 1 :]
                peak = jnp.maximum(peak, old_peak)
                shrink = jnp.exp2(old_peak - peak)
            w = jnp.exp2(s - peak).astype(jnp.bfloat16)
            acc = jnp.dot(w, v_ref[...], preferred_element_type=jnp.float32)
            if has_state:
                acc = acc + old * shrink
            if mode == "state":
                out[h, :, :HD] = acc[:, :HD]
                out[h, :, HD:] = jnp.where(lanes < HD // 2, acc[:, HD:], peak)
            else:
                total = acc[:, HD:]
                if has_state:
                    total = jnp.where(lanes < HD // 2, total, pltpu.roll(total, HD // 2, 1))
                out[:, pl.ds(at, HD)] = (acc[:, :HD] / total).astype(out.dtype)
                lse = peak + jnp.log2(total)
                stat = stat_ref[...]
                if mode == "home":
                    stat = jnp.where(lanes == h, lse, stat)
                else:
                    hi = lse.astype(jnp.bfloat16).astype(jnp.float32)
                    mid = (lse - hi).astype(jnp.bfloat16).astype(jnp.float32)
                    for part, off in ((hi, 0), (mid, heads), (lse - hi - mid, 2 * heads)):
                        stat = jnp.where(lanes == h + off, part, stat)
                stat_ref[...] = stat

        def some_heads(g, carry):
            for u in range(unroll):
                one_head(g * unroll + u)
            return carry

        lax.fori_loop(0, heads // unroll, some_heads, 0)
        if mode != "state":
            out[:, heads * HD :] = stat_ref[...].astype(out.dtype)

    args = [q]
    if has_state:
        args.append(state)
    if lead:
        args.append(fresh)
    args += [arr for arr, _ in pieces]
    whole = pl.BlockSpec(memory_space=pltpu.VMEM)
    if mode != "state":
        kind = jnp.float32 if mode == "home" else jnp.bfloat16
        out_shape = jax.ShapeDtypeStruct((rows, (heads + 1) * HD), kind)
    else:
        out_shape = jax.ShapeDtypeStruct((heads, rows, 2 * HD), jnp.float32)
    return pl.pallas_call(
        body,
        in_specs=[pl.BlockSpec(memory_space=pltpu.SMEM)] + [whole] * len(args),
        out_specs=whole,
        scratch_shapes=[
            pltpu.VMEM((nkv * PAGE, HD), jnp.bfloat16),
            pltpu.VMEM((nkv * PAGE, 2 * HD), jnp.bfloat16),
            pltpu.VMEM((rows, HD), jnp.float32),
        ],
        out_shape=out_shape,
        input_output_aliases={2: 0} if has_state and mode == "state" else {},
        compiler_params=pltpu.CompilerParams(vmem_limit_bytes=16 << 20),
    )(lims, *args)


def merge(home, parts):
    rows = home.shape[0]
    heads = home.shape[1] // HD - 1

    def body(home_ref, *refs):
        part_refs, out = refs[:-1], refs[-1]
        lses = [home_ref[:, heads * HD :]]
        for p in part_refs:
            st = p[:, heads * HD :].astype(jnp.float32)
            lses.append(
                st + pltpu.roll(st, HD - heads, 1) + pltpu.roll(st, HD - 2 * heads, 1)
            )
        top = lses[0]
        for lse in lses[1:]:
            top = jnp.maximum(top, lse)
        ws = [jnp.exp2(lse - top) for lse in lses]
        total = ws[0]
        for w in ws[1:]:
            total = total + w
        ws = [w / total for w in ws]
        for h in range(heads):
            cut = slice(h * HD, (h + 1) * HD)
            acc = home_ref[:, cut] * ws[0][:, h : h + 1]
            for p, w in zip(part_refs, ws[1:]):
                acc = acc + p[:, cut].astype(jnp.float32) * w[:, h : h + 1]
            out[:, cut] = acc.astype(jnp.bfloat16)

    whole = pl.BlockSpec(memory_space=pltpu.VMEM)
    return pl.pallas_call(
        body,
        in_specs=[whole] * (1 + len(parts)),
        out_specs=whole,
        out_shape=jax.ShapeDtypeStruct((rows, heads * HD), jnp.bfloat16),
        compiler_params=pltpu.CompilerParams(vmem_limit_bytes=16 << 20),
    )(home, *parts)


def shift(x, dy, dz):
    pairs = [
        (s, ((s // NZ + dy) % NY) * NZ + (s % NZ + dz) % NZ) for s in range(NY * NZ)
    ]
    return lax.ppermute(x, "pool", pairs)


ROWS = (1, 3, 2)


def on_device(queries, new_kv, pool, page_owner, page_slot, cached_len):
    me = lax.axis_index("pool")
    y = me >> 3
    z = me & (NZ - 1)
    q = queries[0]
    i32 = jnp.int32

    q_up = shift(q, 0, 1)

    goal = [(dy, -4) for dy in range(NY)] + [(dy, 3) for dy in range(NY)]
    goal += [(dy, e) for dy in ROWS for e in (-2, 1, 0, -1)]
    goal += [(0, e) for e in (-2, 1, 0, -1)]
    goal += [(dy, e) for dy in ROWS for e in (-3, 2)] + [(0, -3), (0, 2)]
    goal = jnp.array(goal, i32)
    goal_req = ((y + goal[:, 0]) & (NY - 1)) * NZ + ((z + goal[:, 1]) & (NZ - 1))
    slot_of = jnp.sum(jnp.where(page_owner == me, page_slot, 0), axis=1)
    pick = goal_req[:, None] == jnp.arange(NY * NZ, dtype=i32)[None, :]
    slots = jnp.sum(jnp.where(pick, slot_of[None, :], 0), axis=1)

    rows = (0,) + ROWS
    use = [(role, -dy, 0) for role in (0, 1) for dy in rows]
    use += [(1, -dy, dz) for dz in (3, 1) for dy in rows]
    use += [(1, -dy, 2) for dy in rows]
    use += [(0, -dy, dz) for dz in (-3, -1) for dy in rows]
    use += [(0, -dy, -2) for dy in rows]
    table = jnp.array(use, i32)
    upper = table[:, 0] == 1
    owner = ((y + table[:, 1]) & (NY - 1)) * NZ + ((z + table[:, 2]) & (NZ - 1))
    below = y * NZ + ((z - 1) & (NZ - 1))

    def both(array):
        own = lax.dynamic_index_in_dim(array, me, 0, keepdims=True)
        other = lax.dynamic_index_in_dim(array, below, 0, keepdims=True)
        return jnp.where(upper.reshape((-1,) + (1,) * (own.ndim - 1)), other, own)

    number = jnp.arange(page_owner.shape[1], dtype=i32)[None, :]
    page_no = jnp.sum(jnp.where(both(page_owner) == owner[:, None], number, 0), axis=1)
    lims = jnp.clip(both(cached_len) - PAGE * page_no, 0, PAGE).astype(i32)

    m3, p3 = gather_pages(pool, slots, 0, (4, 4))
    far_m, far_p = shift(m3, 0, -3), shift(p3, 0, 3)
    *side_b, own_b = gather_pages(pool, slots, 8, (4, 4, 4, 4))
    b = [shift(x, dy, 0) for dy, x in zip(ROWS, side_b)]
    *side_a, own_a = gather_pages(pool, slots, 24, (2, 2, 2, 2))
    a = [shift(x, dy, 0) for dy, x in zip(ROWS, side_a)]

    m1, p1 = bundles([own_b] + b, ((0,), (1,)))
    m1, p1 = shift(m1, 0, -1), shift(p1, 0, 1)
    on = bundles([far_m, far_p], [((0, dy), (1, dy)) for dy in ROWS])
    f = [shift(x, dy, 0) for dy, x in zip(ROWS, on)]
    m2, p2 = bundles([own_a] + a, ((0,), (1,)))
    m2, p2 = shift(m2, 0, -2), shift(p2, 0, 2)

    four = [0, 1, 2, 3]
    low = [(own_b, [2])] + [(x, [2]) for x in b]
    upp = [(own_b, [3])] + [(x, [3]) for x in b]
    up = attend(q_up, None, lims, 4, upp, None, "state", unroll=2)
    home = attend(q, None, lims, 0, low, new_kv[0], "state", unroll=2)
    up = attend(
        q_up, up, lims, 8, [(far_m, [0])] + [(x, [0]) for x in f] + [(m1, four)], None, "state"
    )
    up = attend(q_up, up, lims, 16, [(m2, four)], None, "partial")
    back = shift(up, 0, -1)
    home = attend(
        q, home, lims, 20, [(far_p, [0])] + [(x, [1]) for x in f] + [(p1, four)], None, "state"
    )
    home = attend(q, home, lims, 28, [(p2, four)], None, "home", unroll=4)
    return merge(home, [back])[None]


def solution(mesh):
    split = P("pool", None, "head")
    return jax.shard_map(
        on_device,
        mesh=mesh,
        in_specs=(split, split, split, P(), P(), P()),
        out_specs=split,
        check_vma=False,
    )
```

```python
import math

import jax
import jax.numpy as jnp
from jax import lax
from jax.experimental import pallas as pl
from jax.experimental.pallas import tpu as pltpu
from jax.sharding import PartitionSpec as P


HD = 128
PAGE = 256
NY = 4
NZ = 8
SCALE = math.log2(math.e) / math.sqrt(HD)
MASKED = -1e30


def gather_pages(pool, slots, base, counts):
    def body(slot_ref, pool_ref, *outs):
        places = [(out, i) for out, count in zip(outs, counts) for i in range(count)]
        for k, (out, i) in enumerate(places):
            out[i] = pool_ref[slot_ref[base + k]]

    whole = pl.BlockSpec(memory_space=pltpu.VMEM)
    return pl.pallas_call(
        body,
        in_specs=[pl.BlockSpec(memory_space=pltpu.SMEM), whole],
        out_specs=[whole] * len(counts),
        out_shape=[jax.ShapeDtypeStruct((c,) + pool.shape[1:], pool.dtype) for c in counts],
        compiler_params=pltpu.CompilerParams(vmem_limit_bytes=4 << 20),
    )(slots, pool)


def bundles(arrays, plans):
    plans = [
        [(i, p[0]) for i in range(len(arrays))] if len(p) == 1 else list(p) for p in plans
    ]

    def body(*refs):
        ins, outs = refs[: len(arrays)], refs[len(arrays) :]
        for out, plan in zip(outs, plans):
            for at, (i, k) in enumerate(plan):
                out[at] = ins[i][k]

    whole = pl.BlockSpec(memory_space=pltpu.VMEM)
    return pl.pallas_call(
        body,
        in_specs=[whole] * len(arrays),
        out_specs=[whole] * len(plans),
        out_shape=[
            jax.ShapeDtypeStruct((len(p),) + arrays[0].shape[1:], arrays[0].dtype) for p in plans
        ],
        compiler_params=pltpu.CompilerParams(vmem_limit_bytes=4 << 20),
    )(*arrays)


def attend(q, state, lims, base, pieces, fresh, mode, unroll=8):
    heads = q.shape[1] // HD
    rows = q.shape[0]
    npg = sum(len(ids) for _, ids in pieces)
    lead = 1 if fresh is not None else 0
    nkv = npg + lead
    has_state = state is not None

    def body(lim_ref, q_ref, *refs):
        refs = list(refs)
        st_in = refs.pop(0) if has_state else None
        fr = refs.pop(0) if lead else None
        pgs = [refs.pop(0) for _ in pieces]
        out = refs.pop(0)
        k_ref, v_ref, stat_ref = refs
        v_ref[:, HD:] = jnp.ones((nkv * PAGE, HD), jnp.bfloat16)
        blocks = [fr[...]] if lead else []
        for pg, (_, ids) in zip(pgs, pieces):
            blocks += [pg[i] for i in ids]
        for i, blk in enumerate(blocks):
            at = i * PAGE
            k_ref[at : at + PAGE] = blk[:, :HD]
            v_ref[at : at + PAGE, :HD] = blk[:, HD:]
        lane = lax.broadcasted_iota(jnp.int32, (1, PAGE), 1)
        bias = [jnp.where(lane < lim_ref[base + i], 0.0, MASKED) for i in range(npg)]
        lanes = lax.broadcasted_iota(jnp.int32, (rows, HD), 1)
        if mode != "state":
            stat_ref[...] = jnp.zeros((rows, HD), jnp.float32)

        def one_head(h):
            at = pl.multiple_of(h * HD, HD)
            qh = q_ref[:, pl.ds(at, HD)]
            s = lax.dot_general(
                qh, k_ref[...], (((1,), (1,)), ((), ())), preferred_element_type=jnp.float32
            )
            cols = []
            for i in range(nkv):
                c = s[:, i * PAGE : (i + 1) * PAGE] * SCALE
                if i < lead:
                    r_i = lax.broadcasted_iota(jnp.int32, (rows, PAGE), 0)
                    c_i = lax.broadcasted_iota(jnp.int32, (rows, PAGE), 1)
                    c = jnp.where(c_i <= r_i, c, MASKED)
                else:
                    c = c + bias[i - lead]
                cols.append(c)
            s = jnp.concatenate(cols, axis=1) if nkv > 1 else cols[0]
            peak = jnp.max(s, axis=-1, keepdims=True)
            if has_state:
                old = st_in[h]
                old_peak = old[:, 2 * HD - 1 :]
                peak = jnp.maximum(peak, old_peak)
                shrink = jnp.exp2(old_peak - peak)
            w = jnp.exp2(s - peak).astype(jnp.bfloat16)
            acc = jnp.dot(w, v_ref[...], preferred_element_type=jnp.float32)
            if has_state:
                acc = acc + old * shrink
            if mode == "state":
                out[h, :, :HD] = acc[:, :HD]
                out[h, :, HD:] = jnp.where(lanes < HD // 2, acc[:, HD:], peak)
            else:
                total = acc[:, HD:]
                if has_state:
                    total = jnp.where(lanes < HD // 2, total, pltpu.roll(total, HD // 2, 1))
                out[:, pl.ds(at, HD)] = (acc[:, :HD] / total).astype(out.dtype)
                lse = peak + jnp.log2(total)
                stat = stat_ref[...]
                if mode == "home":
                    stat = jnp.where(lanes == h, lse, stat)
                else:
                    hi = lse.astype(jnp.bfloat16).astype(jnp.float32)
                    mid = (lse - hi).astype(jnp.bfloat16).astype(jnp.float32)
                    for part, off in ((hi, 0), (mid, heads), (lse - hi - mid, 2 * heads)):
                        stat = jnp.where(lanes == h + off, part, stat)
                stat_ref[...] = stat

        def some_heads(g, carry):
            for u in range(unroll):
                one_head(g * unroll + u)
            return carry

        lax.fori_loop(0, heads // unroll, some_heads, 0)
        if mode != "state":
            out[:, heads * HD :] = stat_ref[...].astype(out.dtype)

    args = [q]
    if has_state:
        args.append(state)
    if lead:
        args.append(fresh)
    args += [arr for arr, _ in pieces]
    whole = pl.BlockSpec(memory_space=pltpu.VMEM)
    if mode != "state":
        kind = jnp.float32 if mode == "home" else jnp.bfloat16
        out_shape = jax.ShapeDtypeStruct((rows, (heads + 1) * HD), kind)
    else:
        out_shape = jax.ShapeDtypeStruct((heads, rows, 2 * HD), jnp.float32)
    return pl.pallas_call(
        body,
        in_specs=[pl.BlockSpec(memory_space=pltpu.SMEM)] + [whole] * len(args),
        out_specs=whole,
        scratch_shapes=[
            pltpu.VMEM((nkv * PAGE, HD), jnp.bfloat16),
            pltpu.VMEM((nkv * PAGE, 2 * HD), jnp.bfloat16),
            pltpu.VMEM((rows, HD), jnp.float32),
        ],
        out_shape=out_shape,
        input_output_aliases={2: 0} if has_state and mode == "state" else {},
        compiler_params=pltpu.CompilerParams(vmem_limit_bytes=16 << 20),
    )(lims, *args)


def merge(home, parts):
    rows = home.shape[0]
    heads = home.shape[1] // HD - 1

    def body(home_ref, *refs):
        part_refs, out = refs[:-1], refs[-1]
        lses = [home_ref[:, heads * HD :]]
        for p in part_refs:
            st = p[:, heads * HD :].astype(jnp.float32)
            lses.append(
                st + pltpu.roll(st, HD - heads, 1) + pltpu.roll(st, HD - 2 * heads, 1)
            )
        top = lses[0]
        for lse in lses[1:]:
            top = jnp.maximum(top, lse)
        ws = [jnp.exp2(lse - top) for lse in lses]
        total = ws[0]
        for w in ws[1:]:
            total = total + w
        ws = [w / total for w in ws]
        for h in range(heads):
            cut = slice(h * HD, (h + 1) * HD)
            acc = home_ref[:, cut] * ws[0][:, h : h + 1]
            for p, w in zip(part_refs, ws[1:]):
                acc = acc + p[:, cut].astype(jnp.float32) * w[:, h : h + 1]
            out[:, cut] = acc.astype(jnp.bfloat16)

    whole = pl.BlockSpec(memory_space=pltpu.VMEM)
    return pl.pallas_call(
        body,
        in_specs=[whole] * (1 + len(parts)),
        out_specs=whole,
        out_shape=jax.ShapeDtypeStruct((rows, heads * HD), jnp.bfloat16),
        compiler_params=pltpu.CompilerParams(vmem_limit_bytes=16 << 20),
    )(home, *parts)


def shift(x, dy, dz):
    pairs = [
        (s, ((s // NZ + dy) % NY) * NZ + (s % NZ + dz) % NZ) for s in range(NY * NZ)
    ]
    return lax.ppermute(x, "pool", pairs)


ROWS = (1, 3, 2)


def on_device(queries, new_kv, pool, page_owner, page_slot, cached_len):
    me = lax.axis_index("pool")
    y = me >> 3
    z = me & (NZ - 1)
    q = queries[0]
    i32 = jnp.int32

    q_up = shift(q, 0, 1)

    goal = [(dy, -4) for dy in range(NY)] + [(dy, 3) for dy in range(NY)]
    goal += [(dy, e) for dy in ROWS for e in (-2, 1, 0, -1)]
    goal += [(0, e) for e in (-2, 1, 0, -1)]
    goal += [(dy, e) for dy in ROWS for e in (-3, 2)] + [(0, -3), (0, 2)]
    goal = jnp.array(goal, i32)
    goal_req = ((y + goal[:, 0]) & (NY - 1)) * NZ + ((z + goal[:, 1]) & (NZ - 1))
    slot_of = jnp.sum(jnp.where(page_owner == me, page_slot, 0), axis=1)
    pick = goal_req[:, None] == jnp.arange(NY * NZ, dtype=i32)[None, :]
    slots = jnp.sum(jnp.where(pick, slot_of[None, :], 0), axis=1)

    rows = (0,) + ROWS
    use = [(role, -dy, 0) for role in (0, 1) for dy in rows]
    use += [(1, -dy, dz) for dz in (1, 3) for dy in rows]
    use += [(1, -dy, 2) for dy in rows]
    use += [(0, -dy, dz) for dz in (-1, -3) for dy in rows]
    use += [(0, -dy, -2) for dy in rows]
    table = jnp.array(use, i32)
    upper = table[:, 0] == 1
    owner = ((y + table[:, 1]) & (NY - 1)) * NZ + ((z + table[:, 2]) & (NZ - 1))
    below = y * NZ + ((z - 1) & (NZ - 1))

    def both(array):
        own = lax.dynamic_index_in_dim(array, me, 0, keepdims=True)
        other = lax.dynamic_index_in_dim(array, below, 0, keepdims=True)
        return jnp.where(upper.reshape((-1,) + (1,) * (own.ndim - 1)), other, own)

    number = jnp.arange(page_owner.shape[1], dtype=i32)[None, :]
    page_no = jnp.sum(jnp.where(both(page_owner) == owner[:, None], number, 0), axis=1)
    lims = jnp.clip(both(cached_len) - PAGE * page_no, 0, PAGE).astype(i32)

    m3, p3 = gather_pages(pool, slots, 0, (4, 4))
    far_m, far_p = shift(m3, 0, -3), shift(p3, 0, 3)
    *side_b, own_b = gather_pages(pool, slots, 8, (4, 4, 4, 4))
    b = [shift(x, dy, 0) for dy, x in zip(ROWS, side_b)]
    *side_a, own_a = gather_pages(pool, slots, 24, (2, 2, 2, 2))
    a = [shift(x, dy, 0) for dy, x in zip(ROWS, side_a)]

    m1, p1 = bundles([own_b] + b, ((0,), (1,)))
    m1, p1 = shift(m1, 0, -1), shift(p1, 0, 1)
    on = bundles([far_m, far_p], [((0, dy), (1, dy)) for dy in ROWS])
    f = [shift(x, dy, 0) for dy, x in zip(ROWS, on)]
    m2, p2 = bundles([own_a] + a, ((0,), (1,)))
    m2, p2 = shift(m2, 0, -2), shift(p2, 0, 2)

    four = [0, 1, 2, 3]
    low = [(own_b, [2])] + [(x, [2]) for x in b]
    upp = [(own_b, [3])] + [(x, [3]) for x in b]
    upp.append((m1, four))
    home = attend(q, None, lims, 0, low, new_kv[0], "state", unroll=2)
    up = attend(q_up, None, lims, 4, upp, None, "state")
    home = attend(q, home, lims, 20, [(p1, four)], None, "state", unroll=4)
    up = attend(q_up, up, lims, 12, [(far_m, [0])] + [(x, [0]) for x in f], None, "state")
    up = attend(q_up, up, lims, 16, [(m2, four)], None, "partial")
    back = shift(up, 0, -1)
    home = attend(
        q, home, lims, 24, [(far_p, [0])] + [(x, [1]) for x in f], None, "state", unroll=4
    )
    home = attend(q, home, lims, 28, [(p2, four)], None, "home", unroll=4)
    return merge(home, [back])[None]


def solution(mesh):
    split = P("pool", None, "head")
    return jax.shard_map(
        on_device,
        mesh=mesh,
        in_specs=(split, split, split, P(), P(), P()),
        out_specs=split,
        check_vma=False,
    )
```
